256 devices in a mesh: pipe: 8 (over z), expert: 32 (over x, y, core).
Axes of the slice: x: 4, y: 4, z: 8, core: 2. Of those that a mesh axis runs over, the one named last changes fastest.
Arguments:
- inputs: bfloat16 [8, 4096, 4096], P('pipe', 'expert'), may hold values from -6 to 6
- upstream: bfloat16 [8, 4096, 4096], P('pipe', 'expert'), may hold values from -24 to 24
- route: int32 [8, 4096, 8], P('pipe', 'expert'), may hold values from 0 to 127, as said below
- prob: float32 [8, 4096, 8], P('pipe', 'expert'), may hold values from 0.05 to 0.4
- gate_up: bfloat16 [8, 32, 4096, 384], P('pipe', 'expert'), may hold values from -0.09375 to 0.09375
- down: bfloat16 [8, 32, 192, 4096], P('pipe', 'expert'), may hold values from -0.15625 to 0.15625
Outputs:
- grad_input: bfloat16 [8, 4096, 4096], P('pipe', 'expert')
- grad_gate_up: bfloat16 [8, 32, 4096, 384], P('pipe', 'expert')
- grad_down: bfloat16 [8, 32, 192, 4096], P('pipe', 'expert')
The draws below stay inside these ranges and needn't reach their ends.
Inputs may be any that keep to these rules, and one draw needn't show every extreme that they name: `route`: each token names 8 different experts and at most one expert below 4. In each aligned block of 128 tokens of a section every expert below 4 is named by 1 to 8 tokens; one such expert, the same for all blocks, is named by exactly 8 tokens of every block.
All inputs are finite; a program needn't handle non-finite values.
Results may differ from the reference program's by a relative error of at most 0.014.
Values may be sent and summed in bfloat16 or wider, within the bound.
No kernel may reach another device: no remote copies, remote signals or barrier semaphores. Data moves between devices by JAX's collectives and lax.ppermute only.
A program may use at most 128 MiB of HBM per device.

```python
import math
import jax
import jax.numpy as jnp
from jax import lax

D = 4096
H = 1536
EXPERTS = 128
TOPK = 8
SPLIT = 8
CAP = 8
TOK_DEV = 128
HS = 192
EXP_FLIGHT = 4
TOKENS = 4096
N_PIPE = 8
N_EXPERT = 32


def draw_route(key, part):
    keys = jax.random.split(key, 5)
    blocks = N_PIPE * (TOKENS // TOK_DEV)
    flight = EXP_FLIGHT
    hot_one = jax.random.randint(keys[0], (), 0, flight)
    counts = jax.random.randint(keys[1], (blocks, flight), 1, CAP + 1)
    counts = jnp.where(jnp.arange(flight)[None, :] == hot_one, CAP, counts)
    ends = jnp.cumsum(counts, axis=1)
    scores = jax.random.randint(keys[2], (blocks, TOK_DEV), 0, 2 ** 20) * TOK_DEV + jnp.arange(TOK_DEV)[None, :]
    rank = jnp.argsort(jnp.argsort(scores, axis=1, stable=True), axis=1, stable=True).astype(jnp.int32)
    has_one = rank < ends[:, -1:]
    chosen = jnp.sum((rank[:, :, None] >= ends[:, None, :]).astype(jnp.int32), axis=2)
    others_n = EXPERTS - flight
    other_scores = jax.random.randint(keys[3], (blocks, TOK_DEV, others_n), 0, 2 ** 16) * others_n + jnp.arange(others_n)[None, None, :]
    picked = lax.top_k(other_scores, TOPK)[1].astype(jnp.int32) + flight
    where_slot = jax.random.randint(keys[4], (blocks, TOK_DEV), 0, TOPK)
    place = has_one[:, :, None] & (jnp.arange(TOPK)[None, None, :] == where_slot[:, :, None])
    ids = jnp.where(place, chosen[:, :, None], picked)
    return ids.reshape(N_PIPE, TOKENS, TOPK).astype(jnp.int32)


def shard_levels(own_key, extent, cuts, low, top_value):
    gain = 1.0
    for position, parts in cuts:
        steps = jax.random.uniform(jax.random.fold_in(jax.random.fold_in(own_key, 6), position), (parts,), jnp.float32, low / len(cuts), top_value / len(cuts))
        gain = gain * jnp.repeat(jnp.exp(steps), extent[position] // parts).reshape((-1,) + (1,) * (len(extent) - 1 - position))
    return gain


def gaussian(own_key, shape, scale, limit, pieces=(), held_as=jnp.bfloat16):
    entries = jax.random.normal(own_key, shape, jnp.float32) * scale
    if len(pieces) > 0:
        entries = shard_levels(own_key, shape, pieces, -0.22, 0.18) * entries
    return jnp.clip(entries, min=-limit, max=limit).astype(held_as)


def setup_inputs(seed: int = 0) -> dict:
    key_of = jax.random.split(jax.random.key(seed), 7)
    return {
        "inputs": gaussian(key_of[0], (N_PIPE, TOKENS, D), 1.0, 6.0, ((0, 8), (1, 32))),
        "upstream": gaussian(key_of[1], (N_PIPE, TOKENS, D), 4.0, 24.0, ((0, 8), (1, 32))),
        "route": draw_route(jax.random.fold_in(key_of[6], 71), 0),
        "prob": jnp.clip(jnp.exp(math.log(0.4) - 2.0794415 * jax.random.uniform(key_of[3], (N_PIPE, TOKENS, TOPK), jnp.float32) ** shard_levels(key_of[3], (N_PIPE, TOKENS, TOPK), ((0, 8), (1, 32)), -0.2, 0.2)), 0.05, 0.4),
        "gate_up": gaussian(key_of[4], (N_PIPE, N_EXPERT, D, 2 * HS), D ** -0.5, 0.09375, ((0, 8), (1, 32))),
        "down": gaussian(key_of[5], (N_PIPE, N_EXPERT, HS, D), H ** -0.5, 0.15625, ((0, 8), (1, 32))),
    }


def reference(inputs, upstream, route, prob, gate_up, down):
    tokens = inputs.shape[1]
    width = inputs.shape[2]
    blocks = tokens // TOK_DEV
    hidden_cols = down.shape[2]
    slot_ids = jnp.arange(CAP, dtype=jnp.int32)
    grad_inputs = []
    grad_gu_all = []
    grad_down_all = []
    for section in range(N_PIPE):
        arrived = upstream[(section + 1) % N_PIPE].astype(jnp.float32)
        layer_in = inputs[section]
        total = jnp.zeros((tokens, width), jnp.float32)
        gu_rows = []
        dn_rows = []
        for expert in range(EXP_FLIGHT):
            hits = route[section] == expert
            member = jnp.any(hits, axis=1).astype(jnp.int32)
            weight = jnp.sum(jnp.where(hits, prob[section], jnp.float32(0.0)), axis=1)
            member_b = member.reshape(blocks, TOK_DEV)
            rank = jnp.cumsum(member_b, axis=1) - member_b
            select = (member_b[:, None, :] == 1) & (rank[:, None, :] == slot_ids[None, :, None])
            picker = select.astype(jnp.float32)
            x_blocks = layer_in.reshape(blocks, TOK_DEV, width).astype(jnp.float32)
            rows_x = jnp.einsum("bct,btd->bcd", picker, x_blocks, precision=lax.Precision.HIGHEST).reshape(-1, width).astype(jnp.bfloat16)
            scaled = (arrived * weight[:, None]).reshape(blocks, TOK_DEV, width)
            rows_e = jnp.einsum("bct,btd->bcd", picker, scaled, precision=lax.Precision.HIGHEST).reshape(-1, width).astype(jnp.bfloat16)
            part_total = jnp.zeros((blocks * CAP, width), jnp.float32)
            for slice_idx in range(SPLIT):
                row = expert * SPLIT + slice_idx
                w_both = gate_up[section, row]
                w_down = down[section, row]
                both = jnp.dot(rows_x, w_both, preferred_element_type=jnp.float32)
                pre_gate = both[:, :hidden_cols]
                pre_up = both[:, hidden_cols:]
                sigma = jax.nn.sigmoid(pre_gate)
                silu_val = pre_gate * sigma
                hidden = (silu_val * pre_up).astype(jnp.bfloat16)
                grad_hidden = jnp.dot(rows_e, w_down.T, preferred_element_type=jnp.float32)
                grad_a = (grad_hidden * pre_up * sigma * (1.0 + pre_gate * (1.0 - sigma))).astype(jnp.bfloat16)
                grad_u = (grad_hidden * silu_val).astype(jnp.bfloat16)
                grad_both = jnp.concatenate([grad_a, grad_u], axis=1)
                dn_rows.append(jnp.dot(hidden.T, rows_e, preferred_element_type=jnp.float32).astype(jnp.bfloat16))
                gu_rows.append(jnp.dot(rows_x.T, grad_both, preferred_element_type=jnp.float32).astype(jnp.bfloat16))
                part = jnp.dot(grad_both, w_both.T, preferred_element_type=jnp.float32).astype(jnp.bfloat16)
                part_total = part_total + part.astype(jnp.float32)
            back = jnp.einsum("bct,bcd->btd", picker, part_total.reshape(blocks, CAP, width), precision=lax.Precision.HIGHEST)
            total = total + back.reshape(tokens, width)
        grad_inputs.append(total.astype(jnp.bfloat16))
        grad_gu_all.append(jnp.stack(gu_rows))
        grad_down_all.append(jnp.stack(dn_rows))
    return jnp.stack(grad_inputs), jnp.stack(grad_gu_all), jnp.stack(grad_down_all)
```

```python
import functools

import jax
import jax.numpy as jnp
from jax import lax
from jax.experimental import pallas as pl
from jax.experimental.pallas import tpu as pltpu
from jax.sharding import PartitionSpec as P

SPLIT = 8
CAP = 8
VM = pl.BlockSpec(memory_space=pltpu.VMEM)
SM = pl.BlockSpec(memory_space=pltpu.SMEM)
KT = 512
BF = jnp.bfloat16
F32 = jnp.float32


def call(body, outs, flops, nbytes, name):
    return pl.pallas_call(
        body,
        out_shape=outs,
        out_specs=jax.tree.map(lambda _: VM, outs),
        cost_estimate=pl.CostEstimate(flops=flops, bytes_accessed=nbytes, transcendentals=0),
        compiler_params=pltpu.CompilerParams(vmem_limit_bytes=40 << 20),
        name=name,
    )


def slot_table(first, route, prob, flight):
    tokens, topk = route.shape
    cols = flight * CAP
    lane = lax.broadcasted_iota(jnp.int32, (tokens, cols), 1)
    expert = lax.rem(first + lane // CAP, flight)
    hit = jnp.zeros((tokens, cols), jnp.bool_)
    weight = jnp.zeros((tokens, cols), F32)
    for r in range(topk):
        same = route[:, r : r + 1] == expert
        hit = hit | same
        if prob is not None:
            weight = weight + jnp.where(same, prob[:, r : r + 1], F32(0.0))
    member = hit.astype(F32)
    below = lax.broadcasted_iota(jnp.int32, (tokens, tokens), 0) > lax.broadcasted_iota(
        jnp.int32, (tokens, tokens), 1
    )
    rank = jnp.dot(below.astype(BF), member.astype(BF), preferred_element_type=F32)
    taken = hit & (rank.astype(jnp.int32) == lax.rem(lane, CAP))
    return taken, weight


def pick_rows(flight, first_ref, route_ref, prob_ref, data_ref, *outs):
    taken, weight = slot_table(
        first_ref[0], route_ref[...], None if prob_ref is None else prob_ref[...], flight
    )
    picker = taken.astype(F32).T.astype(BF)
    scale = None
    if prob_ref is not None:
        scale = jnp.sum(jnp.where(taken, weight, F32(0.0)).T, axis=1, keepdims=True)
    width = data_ref.shape[1]

    def step(i, _):
        cols = pl.ds(pl.multiple_of(i * KT, KT), KT)
        rows = jnp.dot(picker, data_ref[:, cols], preferred_element_type=F32)
        if scale is not None:
            rows = rows * scale
        for k, out in enumerate(outs):
            out[:, cols] = rows[k * CAP : (k + 1) * CAP].astype(BF)
        return 0

    lax.fori_loop(0, width // KT, step, 0)


def pick_x(flight, first_ref, route_ref, data_ref, *outs):
    pick_rows(flight, first_ref, route_ref, None, data_ref, *outs)


def main_body(n, *refs):
    xs, es = refs[:n], refs[n : 2 * n]
    w_ref, d_ref = refs[2 * n : 2 * n + 2]
    parts = refs[2 * n + 2 : 3 * n + 2]
    hid_ref, gb_ref = refs[3 * n + 2 :]
    width, cols2 = w_ref.shape
    hs = d_ref.shape[0]
    rows = xs[0].shape[0]

    def first(i, acc):
        both, dh = acc
        cols = pl.ds(pl.multiple_of(i * KT, KT), KT)
        x = jnp.concatenate([r[:, cols] for r in xs], axis=0)
        e = jnp.concatenate([r[:, cols] for r in es], axis=0)
        both = both + jnp.dot(x, w_ref[cols, :], preferred_element_type=F32)
        dh = dh + lax.dot_general(
            e, d_ref[:, cols], (((1,), (1,)), ((), ())), preferred_element_type=F32
        )
        return both, dh

    both, dh = lax.fori_loop(
        0, width // KT, first, (jnp.zeros((n * rows, cols2), F32), jnp.zeros((n * rows, hs), F32))
    )
    a, u = both[:, :hs], both[:, hs:]
    sigma = 1.0 / (1.0 + jnp.exp(-a))
    silu = a * sigma
    hid_ref[...] = (silu * u).astype(BF)
    da = dh * u * sigma * (1.0 + a * (1.0 - sigma))
    du = dh * silu
    gb_ref[...] = jnp.concatenate([da, du], axis=1).astype(BF)

    def second(i, _):
        cols = pl.ds(pl.multiple_of(i * KT, KT), KT)
        part = lax.dot_general(
            gb_ref[...], w_ref[cols, :], (((1,), (1,)), ((), ())), preferred_element_type=F32
        )
        for j, out in enumerate(parts):
            out[:, cols] = part[j * rows : (j + 1) * rows].astype(BF)
        return 0

    lax.fori_loop(0, width // KT, second, 0)


def grad_body(n, *refs):
    xs, es = refs[:n], refs[n : 2 * n]
    hid_ref, gb_ref, gu_ref, gd_ref = refs[2 * n :]
    width = xs[0].shape[1]

    def step(i, _):
        cols = pl.ds(pl.multiple_of(i * KT, KT), KT)
        x = jnp.concatenate([r[:, cols] for r in xs], axis=0)
        e = jnp.concatenate([r[:, cols] for r in es], axis=0)
        gu_ref[cols, :] = lax.dot_general(
            x, gb_ref[...], (((0,), (0,)), ((), ())), preferred_element_type=F32
        ).astype(BF)
        gd_ref[:, cols] = lax.dot_general(
            hid_ref[...], e, (((0,), (0,)), ((), ())), preferred_element_type=F32
        ).astype(BF)
        return 0

    lax.fori_loop(0, width // KT, step, 0)


def pair_body(*refs):
    n = len(refs) // 3
    for a, b, o in zip(refs[:n], refs[n : 2 * n], refs[2 * n :]):
        o[...] = (a[...].astype(F32) + b[...].astype(F32)).astype(BF)


def sum_body(n, *refs):
    total = refs[0][...].astype(F32)
    for r in refs[1:n]:
        total = total + r[...].astype(F32)
    for k, o in enumerate(refs[n:]):
        o[...] = total[k * CAP : (k + 1) * CAP].astype(BF)


def spread_body(flight, first_ref, route_ref, *refs):
    rows_refs, out_ref = refs[:-1], refs[-1]
    taken, _ = slot_table(first_ref[0], route_ref[...], None, flight)
    picker = taken.astype(F32).astype(BF)
    width = out_ref.shape[1]

    def step(i, _):
        cols = pl.ds(pl.multiple_of(i * KT, KT), KT)
        rows = jnp.concatenate([r[:, cols].astype(F32) for r in rows_refs], axis=0).astype(BF)
        out_ref[:, cols] = jnp.dot(picker, rows, preferred_element_type=F32).astype(BF)
        return 0

    lax.fori_loop(0, width // KT, step, 0)


def shards(nx, ny, inputs, upstream, route, prob, gate_up, down):
    flight = nx
    pipe = lax.axis_size("pipe")
    width = inputs.shape[2]
    groups = nx * ny * 2
    x_data, e_data = inputs[0], upstream[0]
    w_both, w_down = gate_up[0, 0], down[0, 0]
    cols2, hs = w_both.shape[1], w_down.shape[0]
    first = (lax.axis_index("expert") // (ny * 2)).astype(jnp.int32)[None]

    def at(x, y, c):
        return (x % nx) * ny * 2 + (y % ny) * 2 + c

    cells = [(x, y, c) for x in range(nx) for y in range(ny) for c in range(2)]

    def by_x(v, k):
        return lax.ppermute(v, "expert", [(at(x, y, c), at(x + k, y, c)) for x, y, c in cells])

    def by_y(v, k):
        return lax.ppermute(v, "expert", [(at(x, y, c), at(x, y + k, c)) for x, y, c in cells])

    def by_core(v):
        return lax.ppermute(v, "expert", [(at(x, y, c), at(x, y, 1 - c)) for x, y, c in cells])

    def back_and_x(v, k):
        pairs = [
            (p * groups + at(x, y, c), ((p - 1) % pipe) * groups + at(x + k, y, c))
            for p in range(pipe)
            for x, y, c in cells
        ]
        return lax.ppermute(v, ("pipe", "expert"), pairs)

    ahead = [(p, (p + 1) % pipe) for p in range(pipe)]
    far_route = lax.ppermute(route, "pipe", ahead)[0]
    far_prob = lax.ppermute(prob, "pipe", ahead)[0]

    small = jax.ShapeDtypeStruct((CAP, width), BF)

    def specs(n):
        return [SM] + [VM] * n

    def pick(body, outs, n, name):
        return pl.pallas_call(
            body,
            out_shape=outs,
            in_specs=specs(n),
            out_specs=[VM] * len(outs),
            cost_estimate=pl.CostEstimate(flops=1 << 25, bytes_accessed=1 << 21, transcendentals=0),
            name=name,
        )

    x_rows = pick(functools.partial(pick_x, flight), [small] * flight, 2, "pick_x")(
        first, route[0], x_data
    )
    e_rows = pick(functools.partial(pick_rows, flight), [small] * flight, 3, "pick_e")(
        first, far_route, far_prob, e_data
    )
    own_x = jnp.concatenate([x_rows[0]] + [by_x(x_rows[k], k) for k in range(1, flight)], axis=0)
    own_e = jnp.concatenate([back_and_x(e_rows[k], k) for k in range(flight)], axis=0)

    px, mx = by_y(own_x, 1), by_y(own_x, -1)
    ox = by_y(px, 1)
    pe, me = by_y(own_e, 1), by_y(own_e, -1)
    oe = by_y(me, -1)
    near_x, near_e = [own_x, px, mx, ox], [own_e, pe, me, oe]
    xs = near_x + [by_core(v) for v in near_x]
    es = near_e + [by_core(v) for v in near_e]
    n = len(xs)
    rows = n * flight * CAP
    block = jax.ShapeDtypeStruct((flight * CAP, width), BF)
    res = call(
        functools.partial(main_body, n),
        [block] * n
        + [jax.ShapeDtypeStruct((rows, hs), BF), jax.ShapeDtypeStruct((rows, cols2), BF)],
        2 * rows * width * 5 * hs,
        14 << 20,
        "main",
    )(*xs, *es, w_both, w_down)
    parts, hid, gb = res[:n], res[n], res[n + 1]
    other = [by_core(v) for v in parts[n // 2 :]]
    s_own, s_p, s_m, s_o = call(pair_body, [block] * (n // 2), 1 << 20, 3 << 20, "pair")(
        *parts[: n // 2], *other
    )
    grad_gu, grad_down = call(
        functools.partial(grad_body, n),
        [jax.ShapeDtypeStruct((width, cols2), BF), jax.ShapeDtypeStruct((hs, width), BF)],
        2 * rows * width * 3 * hs,
        10 << 20,
        "grads",
    )(*xs, *es, hid, gb)
    sums = call(functools.partial(sum_body, 4), [small] * flight, 1 << 20, 2 << 20, "sum")(
        s_own, by_y(s_p, -1), by_y(s_m, 1), by_y(s_o, 2)
    )
    back = [sums[0]] + [by_x(sums[k], -k) for k in range(1, flight)]
    grad_x = pick(
        functools.partial(spread_body, flight),
        [jax.ShapeDtypeStruct(x_data.shape, BF)],
        1 + flight,
        "spread",
    )(first, route[0], *back)[0]
    return grad_x[None], grad_gu[None, None], grad_down[None, None]


def solution(mesh):
    groups = mesh.shape["expert"]
    nx = groups // SPLIT
    ny = SPLIT // 2
    spec3, spec4 = P("pipe", "expert", None), P("pipe", "expert", None, None)
    return jax.shard_map(
        functools.partial(shards, nx, ny),
        mesh=mesh,
        in_specs=(spec3,) * 4 + (spec4,) * 2,
        out_specs=(spec3, spec4, spec4),
        check_vma=False,
    )
```
